32 devices in a mesh: band: 4 (over z), slab: 8 (over y, x, core).
Axes of the slice: x: 2, y: 2, z: 4, core: 2. Of those that a mesh axis runs over, the one named last changes fastest.
Arguments:
- traces: bfloat16 [8192, 128, 256], P(('slab', 'band')), may hold values from -6 to 6
- data_matrix: bfloat16 [4, 8192, 2, 8192], P('band', None, None, 'slab'), may hold values from -0.099436891 to 0.099436891, as said below
- shot_points: int32 [128], replicated, may hold values from 0 to 8191
- freq_bins: int32 [4], replicated, may hold values from 1 to 127
Outputs:
- multiples: bfloat16 [8192, 128, 256], P(('slab', 'band'))
The draws below stay inside these ranges and needn't reach their ends.
Inputs may be any that keep to these rules, and one draw needn't show every extreme that they name: Reciprocity: data_matrix[f, k, q, r] equals data_matrix[f, r, q, k] for every frequency f, part q and points k, r.
All inputs are finite; a program needn't handle non-finite values.
Results may differ from the reference program's by a relative error of at most 0.008.
Values may be sent and summed in bfloat16 or wider, within the bound.
A program may use at most 256 MiB of HBM per device.

```python
import math
import jax
import jax.numpy as jnp
from jax import lax

NK = 8192
NT = 256
SHOTS = 128
FREQS = 4


def draw_data_matrix(key, part):

    def draw_one(position):
        subkey = jax.random.fold_in(key, position)
        sample = jnp.clip(jax.random.normal(subkey, (NK, 2, NK), jnp.float32), -6.0, 6.0)
        symmetric = (sample + jnp.transpose(sample, (2, 1, 0))) * (0.70710678 / math.sqrt(NK))
        return symmetric.astype(jnp.bfloat16)
    return lax.map(draw_one, jnp.arange(FREQS, dtype=jnp.int32))


def with_ends(array, key, smallest, high):
    index_at = [jax.random.randint(jax.random.fold_in(key, axis), (), 0, length) for axis, length in enumerate(array.shape)]
    main_axis = array.shape.index(max(array.shape))
    beside = index_at[:main_axis] + [(index_at[main_axis] + 1) % array.shape[main_axis]] + index_at[main_axis + 1:]
    return array.at[tuple(index_at)].set(smallest).at[tuple(beside)].set(high)


def block_scale(key, dims, shards, low, high):
    def one(axis_at, shards_of):
        draws = jax.random.uniform(jax.random.fold_in(jax.random.fold_in(key, 6), axis_at), (shards_of,), jnp.float32, low / len(shards), high / len(shards))
        return jnp.repeat(jnp.exp(draws), dims[axis_at] // shards_of).reshape((-1,) + (1,) * (len(dims) - axis_at - 1))

    factor_of = one(*shards[0])
    for cut in shards[1:]:
        factor_of = factor_of * one(*cut)
    return factor_of


def scatter_about(key, extent, scale, reach, cuts=(), held_as=jnp.bfloat16):
    values = jax.random.normal(key, extent, jnp.float32) * scale
    if len(cuts) > 0:
        values = block_scale(key, extent, cuts, -0.22, 0.18) * values
    return jnp.clip(values, min=-reach, max=reach).astype(held_as)


def setup_inputs(seed: int = 0) -> dict:
    arg_keys = jax.random.split(jax.random.key(seed), 5)
    return {
        "traces": scatter_about(arg_keys[0], (NK, SHOTS, NT), 1.0, 6.0, ((0, 32),)),
        "data_matrix": draw_data_matrix(jax.random.fold_in(arg_keys[4], 71), 0),
        "shot_points": with_ends(jax.random.randint(arg_keys[2], (SHOTS,), 0, NK), jax.random.fold_in(arg_keys[2], 1), 0, NK - 1).astype(jnp.int32),
        "freq_bins": with_ends(jax.random.randint(arg_keys[3], (FREQS,), 1, NT // 2), jax.random.fold_in(arg_keys[3], 1), 1, (NT // 2) - 1).astype(jnp.int32),
    }


def tables(freq_bins, samples, factor):
    sample_index = jnp.arange(samples, dtype=jnp.int32)
    phases = freq_bins[:, None] * sample_index[None, :] % samples
    angles = phases.astype(jnp.float32) * (2.0 * math.pi / samples)
    return (jnp.cos(angles) * factor, -jnp.sin(angles) * factor)

def swapped(values):
    half_width = values.shape[-1] // 2
    return jnp.concatenate([-values[..., half_width:], values[..., :half_width]], -1)

def contract(matrix, values):
    real_part = jnp.dot(matrix[:, 0, :].T, values, preferred_element_type=jnp.float32)
    imag_part = jnp.dot(matrix[:, 1, :].T, swapped(values), preferred_element_type=jnp.float32)
    return real_part + imag_part

def reference(traces, data_matrix, shot_points, freq_bins):
    freq_count = FREQS
    cosines, sines = tables(freq_bins, NT, 1.0 / math.sqrt(NT))
    forward = jnp.transpose(jnp.stack([cosines, sines], -1), (1, 0, 2)).reshape(NT, 2 * freq_count).astype(jnp.bfloat16)
    points = jnp.arange(NK, dtype=jnp.int32)
    distance = (points[:, None] - shot_points[None, :]).astype(jnp.float32) / (NK / 8.0)
    aperture = 1.0 / (1.0 + distance * distance)
    transformed = jnp.dot(traces.reshape(NK * SHOTS, NT), forward, preferred_element_type=jnp.float32)
    transformed = transformed.reshape(NK, SHOTS, freq_count, 2) * aperture[:, :, None, None]
    spectra = jnp.transpose(transformed, (0, 2, 3, 1)).reshape(NK, freq_count, 2 * SHOTS).astype(jnp.bfloat16)

    def one_frequency(items):
        matrix, values = items
        first_order = contract(matrix, values).astype(jnp.bfloat16)
        second_order = contract(matrix, first_order)
        return (second_order - first_order.astype(jnp.float32)).astype(jnp.bfloat16)
    combined = lax.map(one_frequency, (data_matrix, jnp.transpose(spectra, (1, 0, 2))))
    cosines, sines = tables(freq_bins, NT, 1.0 / math.sqrt(2.0 * freq_count))
    inverse = jnp.stack([cosines, sines], 1).reshape(2 * freq_count, NT).astype(jnp.bfloat16)
    regrouped = jnp.transpose(combined.reshape(freq_count, NK, 2, SHOTS), (1, 3, 0, 2)).reshape(NK * SHOTS, 2 * freq_count)
    multiples = jnp.dot(regrouped, inverse, preferred_element_type=jnp.float32)
    return multiples.reshape(NK, SHOTS, NT).astype(jnp.bfloat16)
```

```python
import math

import jax
import jax.numpy as jnp
from jax import lax
from jax.experimental import pallas as pl
from jax.experimental.pallas import tpu as pltpu
from jax.sharding import PartitionSpec as P

NK = 8192
LANES = 128
GROUP = 32
MESH = pl.DeviceIdType.MESH


def tables(freq_bins, samples, factor):
    sample_index = jnp.arange(samples, dtype=jnp.int32)
    phases = freq_bins[:, None] * sample_index[None, :] % samples
    angles = phases.astype(jnp.float32) * (2.0 * math.pi / samples)
    return (jnp.cos(angles) * factor, -jnp.sin(angles) * factor)


def swapped(values):
    half_width = values.shape[-1] // 2
    return jnp.concatenate([-values[..., half_width:], values[..., :half_width]], -1)


def contract(values, data_matrix):
    matrix_rows = data_matrix[0]
    block_values = lax.all_gather(values, "slab", axis=0, tiled=True)[:, 0, :]
    real_part = lax.dot_general(
        matrix_rows[:, 0, :],
        block_values,
        (((0,), (0,)), ((), ())),
        preferred_element_type=jnp.float32,
    )
    imag_part = lax.dot_general(
        matrix_rows[:, 1, :],
        swapped(block_values),
        (((0,), (0,)), ((), ())),
        preferred_element_type=jnp.float32,
    )
    updated = [real_part + imag_part]
    return jnp.stack(updated, 1)


def small_table(bins_ref, freqs, samples, factor):
    shape = (2 * freqs, samples)
    row = lax.broadcasted_iota(jnp.int32, shape, 0)
    sample = lax.broadcasted_iota(jnp.int32, shape, 1)
    bins = jnp.full(shape, bins_ref[0], jnp.int32)
    for f in range(1, freqs):
        bins = jnp.where(row // 2 == f, bins_ref[f], bins)
    phases = (bins * sample + row % 2 * (samples // 4)) % samples
    return jnp.cos(phases.astype(jnp.float32) * (2.0 * math.pi / samples)) * factor


def forward_kernel(first_ref, bins_ref, traces_ref, shots_ref, out_ref, weights):
    step = pl.program_id(0)
    freqs = out_ref.shape[0]
    samples = traces_ref.shape[-1]
    points = GROUP * 2

    @pl.when(step == 0)
    def _():
        small = small_table(bins_ref, freqs, samples, 1.0 / math.sqrt(samples)).astype(jnp.bfloat16)
        lanes = 2 * GROUP * freqs
        row = lax.broadcasted_iota(jnp.int32, (2 * freqs, lanes), 0)
        lane = lax.broadcasted_iota(jnp.int32, (2 * freqs, lanes), 1)
        repeat = jnp.where(row == lane // (2 * GROUP) * 2 + lane % 2, 1.0, 0.0).astype(jnp.bfloat16)
        table = jnp.dot(small.astype(jnp.float32).T.astype(jnp.bfloat16), repeat, preferred_element_type=jnp.float32).astype(jnp.bfloat16)
        point = lax.broadcasted_iota(jnp.int32, table.shape, 1) // 2 % GROUP
        for j in range(GROUP):
            weights[j * samples : (j + 1) * samples] = jnp.where(point == j, table, jnp.zeros_like(table))

    left = jnp.concatenate(
        [
            jnp.concatenate([traces_ref[j], traces_ref[GROUP + j]], 0)
            for j in range(GROUP)
        ],
        1,
    )
    product = jnp.dot(left, weights[...], preferred_element_type=jnp.float32)
    lane = lax.broadcasted_iota(jnp.int32, (LANES, LANES), 1)
    point = first_ref[0] + step * points + lane // 2
    shots = jnp.broadcast_to(shots_ref[...].astype(jnp.float32), (LANES, LANES)).T
    distance = (point.astype(jnp.float32) - shots) / (NK / 8.0)
    aperture = 1.0 / (1.0 + distance * distance)
    low = lane < LANES // 2
    for f in range(freqs):
        column = product[:, f // 2 * LANES : (f // 2 + 1) * LANES]
        first, second = column[:LANES], column[LANES:]
        if f % 2 == 0:
            tile = jnp.where(low, first, pltpu.roll(second, LANES // 2, 1))
        else:
            tile = jnp.where(low, pltpu.roll(first, LANES // 2, 1), second)
        out_ref[f] = (tile * aperture).astype(jnp.bfloat16)


def forward(traces, freq_bins, shot_points, first_point):
    points, shots, samples = traces.shape
    freqs = freq_bins.shape[0]
    lanes = 2 * GROUP * freqs
    return pl.pallas_call(
        forward_kernel,
        out_shape=jax.ShapeDtypeStruct((freqs, shots, 2 * points), jnp.bfloat16),
        grid=(points // (2 * GROUP),),
        in_specs=[
            pl.BlockSpec(memory_space=pltpu.SMEM),
            pl.BlockSpec(memory_space=pltpu.SMEM),
            pl.BlockSpec((2 * GROUP, shots, samples), lambda i: (i, 0, 0)),
            pl.BlockSpec((1, shots), lambda i: (0, 0)),
        ],
        out_specs=pl.BlockSpec((freqs, shots, 4 * GROUP), lambda i: (0, 0, i)),
        scratch_shapes=[pltpu.VMEM((GROUP * samples, lanes), jnp.bfloat16)],
        compiler_params=pltpu.CompilerParams(vmem_limit_bytes=40 * 1024 * 1024),
    )(first_point.reshape(1), freq_bins, traces, shot_points.reshape(1, shots))


def inverse_kernel(bins_ref, spectra_ref, out_ref, left, table_ref):
    step = pl.program_id(0)
    freqs, points, width = spectra_ref.shape
    shots = width // 2
    groups, span = out_ref.shape[0], out_ref.shape[1]

    @pl.when(step == 0)
    def _():
        for g in range(groups):
            rows = jnp.concatenate(
                [
                    spectra_ref[f, g * GROUP : (g + 1) * GROUP, q * shots : (q + 1) * shots]
                    for f in range(freqs)
                    for q in range(2)
                ],
                0,
            )
            left[g * shots : (g + 1) * shots] = rows.T
        small = small_table(bins_ref, freqs, out_ref.shape[-1], 1.0 / math.sqrt(2.0 * freqs))
        for r in range(2 * freqs):
            table_ref[r * GROUP : (r + 1) * GROUP] = jnp.broadcast_to(
                small[r : r + 1], (GROUP, out_ref.shape[-1])
            ).astype(jnp.bfloat16)

    table = table_ref[...]
    point = lax.broadcasted_iota(jnp.int32, table.shape, 0) % GROUP
    for j in range(span):
        right = jnp.where(point == step * span + j, table, jnp.zeros_like(table))
        product = jnp.dot(left[...], right, preferred_element_type=jnp.float32).astype(jnp.bfloat16)
        for g in range(groups):
            out_ref[g, j] = product[g * shots : (g + 1) * shots]


def inverse(spectra, freq_bins, samples):
    freqs, points, width = spectra.shape
    shots = width // 2
    groups = points // GROUP
    rows = 2 * freqs * GROUP
    span = 4
    out = pl.pallas_call(
        inverse_kernel,
        out_shape=jax.ShapeDtypeStruct((groups, GROUP, shots, samples), jnp.bfloat16),
        grid=(GROUP // span,),
        in_specs=[
            pl.BlockSpec(memory_space=pltpu.SMEM),
            pl.BlockSpec((freqs, points, width), lambda i: (0, 0, 0)),
        ],
        out_specs=pl.BlockSpec((groups, span, shots, samples), lambda i: (0, i, 0, 0)),
        scratch_shapes=[
            pltpu.VMEM((groups * shots, rows), jnp.bfloat16),
            pltpu.VMEM((rows, samples), jnp.bfloat16),
        ],
        compiler_params=pltpu.CompilerParams(vmem_limit_bytes=40 * 1024 * 1024),
    )(freq_bins, spectra)
    return out.reshape(points, shots, samples)


def predict_kernel(
    u_ref, d_ref, out_ref, dv, g, vt, acc, yk, gs,
    tx_sib, rx_sib, tx_far, relay, tx_near, rx_near, pend, own, stage,
    d_sem, loc_sem, ag_send, ag_recv, a2a_send, a2a_recv, sib_send, sib_recv, rs_send, rs_recv,
):
    bands, shots, width = u_ref.shape
    slabs, rows, cols = dv.shape
    pts = width // 2
    hp = pts // 2
    band = lax.axis_index("band")
    me = lax.axis_index("slab")
    core = lax.rem(me, 2)
    to_sib = 1 - 2 * core
    to_x = 2 - 4 * lax.rem(me // 2, 2)
    to_y = 4 - 8 * (me // 4)
    sib, xn, yn, dn = me + to_sib, me + to_x, me + to_y, me + to_x + to_y
    xs, ys, ds = xn + to_sib, yn + to_sib, dn + to_sib
    upper = band // 2
    nearest = [band, band + 1 - 2 * lax.rem(band, 2), 2 - upper, 3 - 3 * upper]
    farthest = nearest[::-1]
    order = [me, sib, xn, yn, xs, ys, dn, ds]

    barrier = pltpu.get_barrier_semaphore()
    for other in (sib, xn, yn):
        pl.semaphore_signal(barrier, inc=1, device_id={"slab": other}, device_id_type=MESH)
    for other in nearest[1:]:
        pl.semaphore_signal(barrier, inc=1, device_id={"band": other}, device_id_type=MESH)

    flat = d_ref.reshape(slabs * rows, cols)

    def span(at):
        return pl.ds(pl.multiple_of(at * width, width), width)

    def d_copy(at, i):
        slot, p = order[at], nearest[i]
        return pltpu.make_async_copy(
            flat.at[pl.ds(pl.multiple_of(slot * rows + p * width, width), width)],
            dv.at[slot, span(p)],
            d_sem.at[at, i],
        )

    mine = pltpu.make_async_copy(u_ref.at[band], g.at[me, band], loc_sem.at[0])
    mine.start()
    for i in range(bands):
        for at in range(slabs):
            d_copy(at, i).start()
    pl.semaphore_wait(barrier, 3 + bands - 1)

    started = []

    def go(copy):
        copy.start()
        started.append(copy)

    def across(i, source):
        other = nearest[i]
        return pltpu.make_async_remote_copy(
            u_ref.at[other], g.at[me, source], a2a_send.at[0, i], a2a_recv.at[0, source],
            device_id={"band": other}, device_id_type=MESH,
        )

    go(across(1, band))

    def hop(kind, i, slot, where, lo=0, size=shots):
        ref = g.at[slot, nearest[i], pl.ds(lo, size)]
        return pltpu.make_async_remote_copy(
            ref, ref, ag_send.at[kind, i], ag_recv.at[kind, i],
            device_id={"slab": where}, device_id_type=MESH,
        )

    hs = shots // 2

    def send_own(i):
        if i == 0:
            mine.wait()
        else:
            across(i, nearest[i]).wait_recv()
        go(hop(1, i, me, xn))
        go(hop(2, i, me, yn))
        go(hop(0, i, me, sib))

    def forward_near(i):
        hop(1, i, xn, sib).wait_recv()
        go(hop(5, i, xn, yn, 0, hs))
        go(hop(3, i, xn, sib))
        hop(2, i, yn, sib).wait_recv()
        go(hop(7, i, yn, xn, hs, hs))
        go(hop(4, i, yn, sib))

    def forward_far(i):
        hop(5, i, dn, sib, 0, hs).wait_recv()
        hop(7, i, dn, sib, hs, hs).wait_recv()
        go(hop(6, i, dn, sib))

    odd = lax.broadcasted_iota(jnp.int32, (shots, width), 1) % 2 == 1
    begun = []

    def gather_add(pair, i):
        p = nearest[i]
        slots = [order[at] for at in pair]
        for at in pair:
            d_copy(at, i).wait()
        for k, slot in enumerate(slots):
            x = g[slot, p].astype(jnp.float32)
            turned = jnp.where(odd, pltpu.roll(x, 1, 1), pltpu.roll(x, width - 1, 1))
            vt[:shots, k * width : (k + 1) * width] = jnp.where(odd, -x, x).astype(jnp.bfloat16)
            vt[shots:, k * width : (k + 1) * width] = turned.astype(jnp.bfloat16)
        product = jnp.dot(
            vt[...],
            jnp.concatenate([dv[slot, span(p)] for slot in slots], 0),
            preferred_element_type=jnp.float32,
        )
        if begun:
            acc[...] += product
        else:
            acc[...] = product
            begun.append(1)

    def add_own(i):
        hop(0, i, sib, sib).wait_recv()
        gather_add((0, 1), i)

    def add_near(i):
        gather_add((2, 3), i)

    def add_near_sib(i):
        hop(3, i, xs, sib).wait_recv()
        hop(4, i, ys, sib).wait_recv()
        gather_add((4, 5), i)

    def add_far(i):
        hop(6, i, ds, sib).wait_recv()
        gather_add((6, 7), i)

    send_own(0)
    go(across(2, band))
    add_own(0)
    send_own(1)
    go(across(3, band))
    forward_near(0)
    add_near(0)
    add_own(1)
    send_own(2)
    forward_near(1)
    add_near_sib(0)
    add_near(1)
    forward_far(0)
    add_near_sib(1)
    add_own(2)
    forward_near(2)
    add_far(0)
    send_own(3)
    forward_far(1)
    add_near(2)
    add_near_sib(2)
    add_own(3)
    forward_near(3)
    add_far(1)
    add_near(3)
    forward_far(2)
    add_near_sib(3)
    add_far(2)
    forward_far(3)
    add_far(3)

    for c in range(cols // LANES):
        yk[c * LANES : (c + 1) * LANES] = acc[:, c * LANES : (c + 1) * LANES].T.astype(jnp.bfloat16)

    def partial(buffer, slots, n):
        product = jnp.dot(
            jnp.concatenate([dv[slot, span(n)] for slot in slots], 0),
            yk[...],
            preferred_element_type=jnp.float32,
        )
        gs[buffer, 0] = product[:, :LANES]
        gs[buffer, 1] = product[:, LANES:]

    def joined(buffer, k, half):
        at = k * width + half * pts
        even, later = pl.ds(at, hp, stride=2), pl.ds(at + 1, hp, stride=2)
        return jnp.concatenate(
            [
                gs[buffer, 0, even] - gs[buffer, 1, later],
                gs[buffer, 1, even] + gs[buffer, 0, later],
            ],
            1,
        )

    halves = [pl.ds(0, hp), pl.ds(hp, hp)]

    def to_slab(src, dst, sends, recvs, where):
        return pltpu.make_async_remote_copy(
            src, dst, sends, recvs, device_id={"slab": where}, device_id_type=MESH
        )

    def swap(i, k):
        return to_slab(tx_sib.at[i, k], rx_sib.at[i, k], sib_send.at[i, k], sib_recv.at[i, k], sib)

    def far(axis, i):
        return to_slab(
            tx_far.at[i, halves[axis]], relay.at[axis, i],
            rs_send.at[axis, 0, i], rs_recv.at[axis, 0, i], (xn, yn)[axis],
        )

    def near(axis, half, i):
        return to_slab(
            tx_near.at[axis, i, halves[half]], rx_near.at[axis, i, halves[half]],
            rs_send.at[axis, 1 + half, i], rs_recv.at[axis, 1 + half, i], (xn, yn)[axis],
        )

    def for_sib(i, b, pair):
        partial(b, pair, farthest[i])
        for k in range(2):
            for half in range(2):
                tx_sib[i, 2 * b + k, halves[half]] = joined(b, k, half).astype(jnp.bfloat16)
            go(swap(i, 2 * b + k))

    def with_sib(i, b, k, half):
        return joined(b, k, half) + rx_sib[i, 2 * b + k, halves[half]].astype(jnp.float32)

    def far_and_x(i):
        for_sib(i, 0, (ds, xs))
        partial(0, (dn, xn), farthest[i])
        swap(i, 0).wait_recv()
        for half in range(2):
            tx_far[i, halves[half]] = with_sib(i, 0, 0, half).astype(jnp.bfloat16)
            go(far(half, i))
        swap(i, 1).wait_recv()
        tx_near[0, i, halves[0]] = with_sib(i, 0, 1, 0).astype(jnp.bfloat16)
        go(near(0, 0, i))
        pend[0, i] = with_sib(i, 0, 1, 1)

    def y_and_own(i):
        for_sib(i, 1, (ys, sib))
        partial(1, (yn, me), farthest[i])
        swap(i, 2).wait_recv()
        tx_near[1, i, halves[1]] = with_sib(i, 1, 0, 1).astype(jnp.bfloat16)
        go(near(1, 1, i))
        pend[1, i] = with_sib(i, 1, 0, 0)
        swap(i, 3).wait_recv()
        for half in range(2):
            own[i, halves[half]] = with_sib(i, 1, 1, half)

    def pass_on(i):
        for axis in range(2):
            far(1 - axis, i).wait_recv()
            half = 1 - axis
            tx_near[axis, i, halves[half]] = (
                pend[axis, i] + relay[1 - axis, i].astype(jnp.float32)
            ).astype(jnp.bfloat16)
            go(near(axis, half, i))

    def home(i, source):
        n = farthest[i]
        return pltpu.make_async_remote_copy(
            stage.at[n], out_ref.at[source], a2a_send.at[1, i], a2a_recv.at[1, source],
            device_id={"band": n}, device_id_type=MESH,
        )

    def finish(i):
        n = farthest[i]
        for axis in range(2):
            for half in range(2):
                near(axis, half, i).wait_recv()
        first = yk[pl.ds(pl.multiple_of(n * pts, pts), pts)].astype(jnp.float32)
        total = (
            own[i] + rx_near[0, i].astype(jnp.float32) + rx_near[1, i].astype(jnp.float32) - first
        ).astype(jnp.bfloat16)
        if i == bands - 1:
            out_ref[n] = total
        else:
            stage[n] = total
            go(home(i, band))

    far_and_x(0)
    y_and_own(0)
    far_and_x(1)
    pass_on(0)
    y_and_own(1)
    far_and_x(2)
    pass_on(1)
    y_and_own(2)
    finish(0)
    far_and_x(3)
    pass_on(2)
    y_and_own(3)
    finish(1)
    pass_on(3)
    finish(2)
    finish(3)
    for i in range(bands - 1):
        home(i, farthest[i]).wait_recv()
    for copy in started:
        copy.wait_send()


def predict(spectra, data_matrix, slabs):
    bands, shots, width = spectra.shape
    cols = data_matrix.shape[-1]
    pts = width // 2
    bf, f32 = jnp.bfloat16, jnp.float32
    dma = pltpu.SemaphoreType.DMA
    return pl.pallas_call(
        predict_kernel,
        out_shape=jax.ShapeDtypeStruct((bands, pts, 2 * shots), bf),
        in_specs=[pl.BlockSpec(memory_space=pl.ANY), pl.BlockSpec(memory_space=pl.ANY)],
        out_specs=pl.BlockSpec(memory_space=pltpu.VMEM),
        scratch_shapes=[
            pltpu.VMEM((slabs, bands * width, cols), bf),
            pltpu.VMEM((slabs, bands, shots, width), bf),
            pltpu.VMEM((2 * shots, 2 * width), bf),
            pltpu.VMEM((2 * shots, cols), f32),
            pltpu.VMEM((cols, 2 * shots), bf),
            pltpu.VMEM((2, 2, 2 * width, shots), f32),
            pltpu.VMEM((bands, 4, pts, 2 * shots), bf),
            pltpu.VMEM((bands, 4, pts, 2 * shots), bf),
            pltpu.VMEM((bands, pts, 2 * shots), bf),
            pltpu.VMEM((2, bands, pts // 2, 2 * shots), bf),
            pltpu.VMEM((2, bands, pts, 2 * shots), bf),
            pltpu.VMEM((2, bands, pts, 2 * shots), bf),
            pltpu.VMEM((2, bands, pts // 2, 2 * shots), f32),
            pltpu.VMEM((bands, pts, 2 * shots), f32),
            pltpu.VMEM((bands, pts, 2 * shots), bf),
            dma((slabs, bands)),
            dma((1,)),
            dma((8, bands)),
            dma((8, bands)),
            dma((2, bands)),
            dma((2, bands)),
            dma((bands, 4)),
            dma((bands, 4)),
            dma((2, 3, bands)),
            dma((2, 3, bands)),
        ],
        compiler_params=pltpu.CompilerParams(
            collective_id=0, has_side_effects=True, vmem_limit_bytes=60 * 1024 * 1024
        ),
    )(spectra, data_matrix)


def local(traces, data_matrix, shot_points, freq_bins):
    local_pts, shot_count, samples = traces.shape
    freq_count = freq_bins.shape[0]
    band_count = lax.axis_size("band")
    slab_count = lax.axis_size("slab")
    first_point = (lax.axis_index("slab") * band_count + lax.axis_index("band")) * local_pts
    in_kernel = (
        slab_count == 8
        and band_count == 4
        and freq_count == band_count
        and local_pts == 2 * LANES
        and shot_count == LANES
        and samples == 2 * LANES
        and data_matrix.shape[-1] == band_count * local_pts
    )
    if in_kernel:
        spectra = forward(traces, freq_bins, shot_points, first_point)
        combined = predict(spectra, data_matrix, slab_count)
        return inverse(combined, freq_bins, samples)
    cosines, sines = tables(freq_bins, samples, 1.0 / math.sqrt(samples))
    forward_table = (
        jnp.transpose(jnp.stack([cosines, sines], -1), (1, 0, 2))
        .reshape(samples, 2 * freq_count)
        .astype(jnp.bfloat16)
    )
    points = first_point + jnp.arange(local_pts, dtype=jnp.int32)
    distance = (points[:, None] - shot_points[None, :]).astype(jnp.float32) / (NK / 8.0)
    aperture = 1.0 / (1.0 + distance * distance)
    transformed = jnp.dot(
        traces.reshape(local_pts * shot_count, samples), forward_table, preferred_element_type=jnp.float32
    )
    transformed = (
        transformed.reshape(local_pts, shot_count, freq_count, 2) * aperture[:, :, None, None]
    )
    cosines, sines = tables(freq_bins, samples, 1.0 / math.sqrt(2.0 * freq_count))
    inverse_table = jnp.stack([cosines, sines], 1).reshape(2 * freq_count, samples).astype(jnp.bfloat16)
    spectra = (
        jnp.transpose(transformed, (0, 2, 3, 1))
        .reshape(local_pts, freq_count, 2 * shot_count)
        .astype(jnp.bfloat16)
    )
    banded = lax.all_to_all(spectra, "band", split_axis=1, concat_axis=0, tiled=True)
    first_order = contract(banded, data_matrix).astype(jnp.bfloat16)
    second_order = contract(first_order, data_matrix)
    combined = (second_order - first_order.astype(jnp.float32)).astype(jnp.bfloat16)
    regrouped = lax.all_to_all(combined, "band", split_axis=0, concat_axis=1, tiled=True)
    regrouped = jnp.transpose(
        regrouped.reshape(local_pts, freq_count, 2, shot_count), (0, 3, 1, 2)
    ).reshape(local_pts * shot_count, 2 * freq_count)
    multiples = jnp.dot(regrouped, inverse_table, preferred_element_type=jnp.float32)
    return multiples.reshape(local_pts, shot_count, samples).astype(jnp.bfloat16)


def solution(mesh):
    placed = (P(("slab", "band"), None, None), P("band", None, None, "slab"), P(), P())
    return jax.shard_map(
        local,
        mesh=mesh,
        in_specs=placed,
        out_specs=P(("slab", "band"), None, None),
        check_vma=False,
    )
```

```python
import math

import jax
import jax.numpy as jnp
from jax import lax
from jax.experimental import pallas as pl
from jax.experimental.pallas import tpu as pltpu
from jax.sharding import PartitionSpec as P

NK = 8192
LANES = 128
GROUP = 32
MESH = pl.DeviceIdType.MESH


def tables(freq_bins, samples, factor):
    sample_index = jnp.arange(samples, dtype=jnp.int32)
    phases = freq_bins[:, None] * sample_index[None, :] % samples
    angles = phases.astype(jnp.float32) * (2.0 * math.pi / samples)
    return (jnp.cos(angles) * factor, -jnp.sin(angles) * factor)


def swapped(values):
    half_width = values.shape[-1] // 2
    return jnp.concatenate([-values[..., half_width:], values[..., :half_width]], -1)


def contract(values, data_matrix):
    matrix_rows = data_matrix[0]
    block_values = lax.all_gather(values, "slab", axis=0, tiled=True)[:, 0, :]
    real_part = lax.dot_general(
        matrix_rows[:, 0, :],
        block_values,
        (((0,), (0,)), ((), ())),
        preferred_element_type=jnp.float32,
    )
    imag_part = lax.dot_general(
        matrix_rows[:, 1, :],
        swapped(block_values),
        (((0,), (0,)), ((), ())),
        preferred_element_type=jnp.float32,
    )
    updated = [real_part + imag_part]
    return jnp.stack(updated, 1)


def small_table(bins_ref, freqs, samples, factor):
    shape = (2 * freqs, samples)
    row = lax.broadcasted_iota(jnp.int32, shape, 0)
    sample = lax.broadcasted_iota(jnp.int32, shape, 1)
    bins = jnp.full(shape, bins_ref[0], jnp.int32)
    for f in range(1, freqs):
        bins = jnp.where(row // 2 == f, bins_ref[f], bins)
    phases = (bins * sample + row % 2 * (samples // 4)) % samples
    return jnp.cos(phases.astype(jnp.float32) * (2.0 * math.pi / samples)) * factor


def inverse_kernel(bins_ref, spectra_ref, out_ref, left, table_ref, tiles, sems):
    freqs, points, width = spectra_ref.shape
    shots = width // 2
    groups, samples = out_ref.shape[0], out_ref.shape[-1]
    slots, _, span = tiles.shape[:3]
    small = small_table(bins_ref, freqs, samples, 1.0 / math.sqrt(2.0 * freqs))
    for r in range(2 * freqs):
        table_ref[r * GROUP : (r + 1) * GROUP] = jnp.broadcast_to(
            small[r : r + 1], (GROUP, samples)
        ).astype(jnp.bfloat16)
    for g in range(groups):
        rows = jnp.concatenate(
            [
                spectra_ref[f, g * GROUP : (g + 1) * GROUP, q * shots : (q + 1) * shots]
                for f in range(freqs)
                for q in range(2)
            ],
            0,
        )
        left[g * shots : (g + 1) * shots] = rows.T
    table = table_ref[...]
    point = lax.broadcasted_iota(jnp.int32, table.shape, 0) % GROUP

    def put(step):
        slot = step % slots
        return pltpu.make_async_copy(tiles.at[slot], out_ref.at[:, pl.ds(step * span, span)], sems.at[slot])

    steps = GROUP // span
    for step in range(steps):
        slot = step % slots
        if step >= slots:
            put(step - slots).wait()
        for c in range(0, span, 2):
            right = jnp.concatenate(
                [jnp.where(point == step * span + c + j, table, jnp.zeros_like(table)) for j in range(2)], 1
            )
            product = jnp.dot(left[...], right, preferred_element_type=jnp.float32).astype(jnp.bfloat16)
            for g in range(groups):
                for j in range(2):
                    tiles[slot, g, c + j] = product[g * shots : (g + 1) * shots, j * samples : (j + 1) * samples]
        put(step).start()
    for step in range(steps - slots, steps):
        put(step).wait()


def inverse(spectra, freq_bins, samples):
    freqs, points, width = spectra.shape
    shots = width // 2
    groups = points // GROUP
    rows = 2 * freqs * GROUP
    span, slots = 2, 4
    out = pl.pallas_call(
        inverse_kernel,
        out_shape=jax.ShapeDtypeStruct((groups, GROUP, shots, samples), jnp.bfloat16),
        in_specs=[
            pl.BlockSpec(memory_space=pltpu.SMEM),
            pl.BlockSpec(memory_space=pltpu.VMEM),
        ],
        out_specs=pl.BlockSpec(memory_space=pl.ANY),
        scratch_shapes=[
            pltpu.VMEM((groups * shots, rows), jnp.bfloat16),
            pltpu.VMEM((rows, samples), jnp.bfloat16),
            pltpu.VMEM((slots, groups, span, shots, samples), jnp.bfloat16),
            pltpu.SemaphoreType.DMA((slots,)),
        ],
        compiler_params=pltpu.CompilerParams(vmem_limit_bytes=60 * 1024 * 1024),
    )(freq_bins, spectra)
    return out.reshape(points, shots, samples)


def predict_kernel(
    bins_ref, shots_ref, traces_ref, d_ref, out_ref, dv, u, table, g, vt, acc, yk, gs,
    tx_sib, rx_sib, tx_far, relay, tx_near, rx_near, pend, own, stage,
    t_sem, d_sem, ag_send, ag_recv, a2a_send, a2a_recv, back_send, back_recv, sib_send, sib_recv, rs_send, rs_recv,
):
    bands, _, shots, width = u.shape
    slabs, rows, cols = dv.shape
    samples = traces_ref.shape[-1]
    pts = width
    hp = pts // 2
    band = lax.axis_index("band")
    me = lax.axis_index("slab")
    core = lax.rem(me, 2)
    to_sib = 1 - 2 * core
    to_x = 2 - 4 * lax.rem(me // 2, 2)
    to_y = 4 - 8 * (me // 4)
    sib, xn, yn, dn = me + to_sib, me + to_x, me + to_y, me + to_x + to_y
    xs, ys, ds = xn + to_sib, yn + to_sib, dn + to_sib
    upper = band // 2
    nearest = [band, band + 1 - 2 * lax.rem(band, 2), 2 - upper, 3 - 3 * upper]
    farthest = nearest[::-1]
    order = [me, sib, xn, yn, xs, ys, dn, ds]

    barrier = pltpu.get_barrier_semaphore()
    for other in (sib, xn, yn):
        pl.semaphore_signal(barrier, inc=1, device_id={"slab": other}, device_id_type=MESH)
    for other in nearest[1:]:
        pl.semaphore_signal(barrier, inc=1, device_id={"band": other}, device_id_type=MESH)

    chips = dv.reshape(slabs // 2, 8, rows // 4, cols)
    held = [yn // 2, dn // 2]

    def t_copy(half, group, part):
        return pltpu.make_async_copy(
            traces_ref.at[pl.ds(half * hp + group * GROUP + part * 8, 8)],
            chips.at[held[half], :, pl.ds(group * shots, shots), pl.ds(part * samples, samples)],
            t_sem.at[half, group, part],
        )

    def fetch(half):
        for group in range(4):
            for part in range(4):
                t_copy(half, group, part).start()

    def fetched(half):
        for group in range(4):
            for part in range(4):
                t_copy(half, group, part).wait()

    fetch(0)

    flat = d_ref.reshape(slabs * rows, cols)
    full = 2 * width

    def span(at):
        return pl.ds(pl.multiple_of(at * full, full), full)

    def d_copy(at, i):
        slot, p = order[at], nearest[i]
        return pltpu.make_async_copy(
            flat.at[pl.ds(pl.multiple_of(slot * rows + p * full, full), full)],
            dv.at[slot, span(p)],
            d_sem.at[at, i],
        )

    def load(i, places):
        for at in places:
            d_copy(at, i).start()

    small = small_table(bins_ref, bands, samples, 1.0 / math.sqrt(samples))
    lanes = table.shape[1]
    row = lax.broadcasted_iota(jnp.int32, (2 * bands, lanes), 0)
    lane = lax.broadcasted_iota(jnp.int32, (2 * bands, lanes), 1)
    repeat = jnp.where(row == lane // (2 * GROUP) * 2 + lane % 2, 1.0, 0.0).astype(jnp.bfloat16)
    table[...] = jnp.dot(small.T.astype(jnp.bfloat16), repeat, preferred_element_type=jnp.float32).astype(
        jnp.bfloat16
    )
    shot_rows = jnp.broadcast_to(shots_ref[...].astype(jnp.float32), (LANES, LANES)).T
    low = lax.broadcasted_iota(jnp.int32, (LANES, LANES), 1) < LANES // 2
    inner = lax.broadcasted_iota(jnp.int32, (samples, lanes), 1) // 2 % GROUP
    tall = 4 * shots

    def clear():
        gs[0, :, :tall] = jnp.zeros((2, tall, LANES), jnp.float32)

    def transform(half, low_step, high_step):
        @pl.loop(low_step, high_step)
        def _(step):
            values = table[...]
            left, right = [], []
            for n in range(2):
                at = 2 * step + n
                slot = 2 * held[half] + at // 4
                left.append(dv[slot, pl.ds(pl.multiple_of(at % 4 * tall, tall), tall)])
                for part in range(4):
                    right.append(jnp.where(inner == part * 8 + at, values, jnp.zeros_like(values)))
            product = jnp.dot(
                jnp.concatenate(left, 1), jnp.concatenate(right, 0), preferred_element_type=jnp.float32
            )
            gs[0, 0, :tall] += product[:, :LANES]
            gs[0, 1, :tall] += product[:, LANES:]

    def spectra(half):
        first_point = (me * bands + band) * pts + half * hp
        for n in range(2):
            point = first_point + n * 2 * GROUP + lax.broadcasted_iota(jnp.int32, (LANES, LANES), 1) // 2
            distance = (point.astype(jnp.float32) - shot_rows) / (NK / 8.0)
            aperture = 1.0 / (1.0 + distance * distance)
            for f in range(bands):
                first = gs[0, f // 2, 2 * n * shots : (2 * n + 1) * shots]
                second = gs[0, f // 2, (2 * n + 1) * shots : (2 * n + 2) * shots]
                if f % 2 == 0:
                    tile = jnp.where(low, first, pltpu.roll(second, LANES // 2, 1))
                else:
                    tile = jnp.where(low, pltpu.roll(first, LANES // 2, 1), second)
                u[f, half, :, n * LANES : (n + 1) * LANES] = (tile * aperture).astype(jnp.bfloat16)
        g[me, band, half] = u[band, half]

    started = []

    def go(copy):
        copy.start()
        started.append(copy)

    def across(i, half, source):
        other = nearest[i]
        return pltpu.make_async_remote_copy(
            u.at[other, half], g.at[me, source, half], a2a_send.at[i, half], a2a_recv.at[source, half],
            device_id={"band": other}, device_id_type=MESH,
        )

    def hop(kind, unit, slot, where, lo=0, size=shots):
        i, half = unit
        ref = g.at[slot, nearest[i], half, pl.ds(lo, size)]
        return pltpu.make_async_remote_copy(
            ref, ref, ag_send.at[kind, i, half], ag_recv.at[kind, i, half],
            device_id={"slab": where}, device_id_type=MESH,
        )

    hs = shots // 2

    def send_own(unit):
        i, half = unit
        if i > 0:
            across(i, half, nearest[i]).wait_recv()
        go(hop(1, unit, me, xn))
        go(hop(2, unit, me, yn))
        go(hop(0, unit, me, sib))

    def forward_near(unit):
        hop(1, unit, xn, sib).wait_recv()
        go(hop(5, unit, xn, yn, 0, hs))
        go(hop(3, unit, xn, sib))
        hop(2, unit, yn, sib).wait_recv()
        go(hop(7, unit, yn, xn, hs, hs))
        go(hop(4, unit, yn, sib))

    def forward_far(unit):
        hop(5, unit, dn, sib, 0, hs).wait_recv()
        hop(7, unit, dn, sib, hs, hs).wait_recv()
        go(hop(6, unit, dn, sib))

    odd = lax.broadcasted_iota(jnp.int32, (shots, width), 1) % 2 == 1
    begun = []
    loaded = set()

    def gather_add(pair, unit):
        i, half = unit
        p = nearest[i]
        slots = [order[at] for at in pair]
        for at in pair:
            if (at, i) not in loaded:
                loaded.add((at, i))
                d_copy(at, i).wait()
        for k, slot in enumerate(slots):
            x = g[slot, p, half].astype(jnp.float32)
            turned = jnp.where(odd, pltpu.roll(x, 1, 1), pltpu.roll(x, width - 1, 1))
            vt[:shots, k * width : (k + 1) * width] = jnp.where(odd, -x, x).astype(jnp.bfloat16)
            vt[shots:, k * width : (k + 1) * width] = turned.astype(jnp.bfloat16)
        part = pl.ds(pl.multiple_of(p * full + half * width, width), width)
        product = jnp.dot(
            vt[...],
            jnp.concatenate([dv[slot, part] for slot in slots], 0),
            preferred_element_type=jnp.float32,
        )
        if begun:
            acc[...] += product
        else:
            acc[...] = product
            begun.append(1)

    def add_own(unit):
        hop(0, unit, sib, sib).wait_recv()
        gather_add((0, 1), unit)

    def add_near(unit):
        gather_add((2, 3), unit)

    def add_near_sib(unit):
        hop(3, unit, xs, sib).wait_recv()
        hop(4, unit, ys, sib).wait_recv()
        gather_add((4, 5), unit)

    def add_far(unit):
        hop(6, unit, ds, sib).wait_recv()
        gather_add((6, 7), unit)

    units = [(0, 0), (1, 0), (0, 1), (2, 0), (1, 1), (3, 0), (2, 1), (3, 1)]

    clear()
    fetched(0)
    fetch(1)
    transform(0, 0, 2)
    load(0, (0, 1, 2, 4))
    transform(0, 2, 4)
    spectra(0)
    load(0, (3, 5))
    pl.semaphore_wait(barrier, 3 + bands - 1)
    go(across(1, 0, band))
    send_own(units[0])
    go(across(2, 0, band))
    clear()
    fetched(1)
    transform(1, 0, 3)
    forward_near(units[0])
    go(across(3, 0, band))
    send_own(units[1])
    transform(1, 3, 4)
    spectra(1)
    go(across(1, 1, band))
    go(across(2, 1, band))
    send_own(units[2])
    load(0, (6, 7))
    load(1, (0, 1, 2, 3, 4, 5, 6, 7))
    add_own(units[0])
    add_near(units[0])
    forward_near(units[1])
    go(across(3, 1, band))
    forward_far(units[0])
    load(2, (0, 1, 2, 3, 4, 5, 6, 7))
    add_near_sib(units[0])
    add_own(units[1])
    load(3, (0, 1, 2, 3, 4, 5, 6, 7))
    add_near(units[1])
    count = len(units)
    for k in range(3, count + 3):
        if k < count:
            send_own(units[k])
        if k <= count:
            add_own(units[k - 1])
        add_far(units[k - 3])
        if k <= count:
            forward_near(units[k - 1])
            add_near(units[k - 1])
        if k <= count + 1:
            forward_far(units[k - 2])
            add_near_sib(units[k - 2])

    for c in range(cols // LANES):
        yk[c * LANES : (c + 1) * LANES] = acc[:, c * LANES : (c + 1) * LANES].T.astype(jnp.bfloat16)

    def partial(buffer, slots, n):
        product = jnp.dot(
            jnp.concatenate([dv[slot, span(n)] for slot in slots], 0),
            yk[...],
            preferred_element_type=jnp.float32,
        )
        gs[buffer, 0] = product[:, :LANES]
        gs[buffer, 1] = product[:, LANES:]

    def joined(buffer, k, half):
        at = k * full + half * pts
        even, later = pl.ds(at, hp, stride=2), pl.ds(at + 1, hp, stride=2)
        return jnp.concatenate(
            [
                gs[buffer, 0, even] - gs[buffer, 1, later],
                gs[buffer, 1, even] + gs[buffer, 0, later],
            ],
            1,
        )

    halves = [pl.ds(0, hp), pl.ds(hp, hp)]

    def to_slab(src, dst, sends, recvs, where):
        return pltpu.make_async_remote_copy(
            src, dst, sends, recvs, device_id={"slab": where}, device_id_type=MESH
        )

    def swap(i, k):
        return to_slab(tx_sib.at[i, k], rx_sib.at[i, k], sib_send.at[i, k], sib_recv.at[i, k], sib)

    def far(axis, i):
        return to_slab(
            tx_far.at[i, halves[axis]], relay.at[axis, i],
            rs_send.at[axis, 0, i], rs_recv.at[axis, 0, i], (xn, yn)[axis],
        )

    def near(axis, half, i):
        return to_slab(
            tx_near.at[axis, i, halves[half]], rx_near.at[axis, i, halves[half]],
            rs_send.at[axis, 1 + half, i], rs_recv.at[axis, 1 + half, i], (xn, yn)[axis],
        )

    def give(i, b, k, kind):
        for half in range(2):
            tx_sib[i, kind, halves[half]] = joined(b, k, half).astype(jnp.bfloat16)
        go(swap(i, kind))

    def with_sib(i, b, k, kind, half):
        return joined(b, k, half) + rx_sib[i, kind, halves[half]].astype(jnp.float32)

    def first_pair(i):
        partial(0, (ds, xs), farthest[i])
        give(i, 0, 0, 0)
        give(i, 0, 1, 1)

    def second_pair(i):
        partial(1, (ys, dn), farthest[i])
        give(i, 1, 0, 2)
        swap(i, 0).wait_recv()
        for half in range(2):
            tx_far[i, halves[half]] = with_sib(i, 1, 1, 0, half).astype(jnp.bfloat16)
            go(far(half, i))

    def third_pair(i):
        partial(0, (xn, yn), farthest[i])
        for axis in range(2):
            swap(i, 1 + axis).wait_recv()
            tx_near[axis, i, halves[axis]] = with_sib(i, 0, axis, 1 + axis, axis).astype(jnp.bfloat16)
            go(near(axis, axis, i))
            pend[axis, i] = with_sib(i, 0, axis, 1 + axis, 1 - axis)

    def own_pair(i):
        partial(1, (sib, me), farthest[i])
        give(i, 1, 0, 3)
        for half in range(2):
            own[i, halves[half]] = joined(1, 1, half)

    def pass_on(i):
        for axis in range(2):
            far(1 - axis, i).wait_recv()
            half = 1 - axis
            tx_near[axis, i, halves[half]] = (
                pend[axis, i] + relay[1 - axis, i].astype(jnp.float32)
            ).astype(jnp.bfloat16)
            go(near(axis, half, i))

    def home(i, source):
        n = farthest[i]
        return pltpu.make_async_remote_copy(
            stage.at[n], out_ref.at[source], back_send.at[i], back_recv.at[source],
            device_id={"band": n}, device_id_type=MESH,
        )

    def finish(i):
        n = farthest[i]
        for axis in range(2):
            for half in range(2):
                near(axis, half, i).wait_recv()
        swap(i, 3).wait_recv()
        first = yk[pl.ds(pl.multiple_of(n * pts, pts), pts)].astype(jnp.float32)
        total = (
            own[i] + rx_sib[i, 3].astype(jnp.float32) + rx_near[0, i].astype(jnp.float32) + rx_near[1, i].astype(jnp.float32) - first
        ).astype(jnp.bfloat16)
        if i == bands - 1:
            out_ref[n] = total
        else:
            stage[n] = total
            go(home(i, band))

    first_pair(0)
    second_pair(0)
    third_pair(0)
    first_pair(1)
    second_pair(1)
    pass_on(0)
    third_pair(1)
    own_pair(0)
    first_pair(2)
    second_pair(2)
    pass_on(1)
    finish(0)
    third_pair(2)
    own_pair(1)
    first_pair(3)
    second_pair(3)
    pass_on(2)
    finish(1)
    third_pair(3)
    own_pair(2)
    pass_on(3)
    finish(2)
    own_pair(3)
    finish(3)
    for i in range(bands - 1):
        home(i, farthest[i]).wait_recv()
    for copy in started:
        copy.wait_send()


def predict(traces, data_matrix, shot_points, freq_bins, slabs):
    points, shots, samples = traces.shape
    bands = freq_bins.shape[0]
    cols = data_matrix.shape[-1]
    width = points
    pts = points
    bf, f32 = jnp.bfloat16, jnp.float32
    dma = pltpu.SemaphoreType.DMA
    return pl.pallas_call(
        predict_kernel,
        out_shape=jax.ShapeDtypeStruct((bands, pts, 2 * shots), bf),
        in_specs=[
            pl.BlockSpec(memory_space=pltpu.SMEM),
            pl.BlockSpec(memory_space=pltpu.VMEM),
            pl.BlockSpec(memory_space=pl.ANY),
            pl.BlockSpec(memory_space=pl.ANY),
        ],
        out_specs=pl.BlockSpec(memory_space=pltpu.VMEM),
        scratch_shapes=[
            pltpu.VMEM((slabs, 2 * bands * width, cols), bf),
            pltpu.VMEM((bands, 2, shots, width), bf),
            pltpu.VMEM((samples, 2 * bands * GROUP), bf),
            pltpu.VMEM((slabs, bands, 2, shots, width), bf),
            pltpu.VMEM((2 * shots, 2 * width), bf),
            pltpu.VMEM((2 * shots, cols), f32),
            pltpu.VMEM((cols, 2 * shots), bf),
            pltpu.VMEM((2, 2, 4 * pts, shots), f32),
            pltpu.VMEM((bands, 4, pts, 2 * shots), bf),
            pltpu.VMEM((bands, 4, pts, 2 * shots), bf),
            pltpu.VMEM((bands, pts, 2 * shots), bf),
            pltpu.VMEM((2, bands, pts // 2, 2 * shots), bf),
            pltpu.VMEM((2, bands, pts, 2 * shots), bf),
            pltpu.VMEM((2, bands, pts, 2 * shots), bf),
            pltpu.VMEM((2, bands, pts // 2, 2 * shots), f32),
            pltpu.VMEM((bands, pts, 2 * shots), f32),
            pltpu.VMEM((bands, pts, 2 * shots), bf),
            dma((2, 4, 4)),
            dma((slabs, bands)),
            dma((8, bands, 2)),
            dma((8, bands, 2)),
            dma((bands, 2)),
            dma((bands, 2)),
            dma((bands,)),
            dma((bands,)),
            dma((bands, 4)),
            dma((bands, 4)),
            dma((2, 3, bands)),
            dma((2, 3, bands)),
        ],
        compiler_params=pltpu.CompilerParams(
            collective_id=0, has_side_effects=True, vmem_limit_bytes=60 * 1024 * 1024
        ),
    )(freq_bins, shot_points.reshape(1, shots), traces, data_matrix)


def local(traces, data_matrix, shot_points, freq_bins):
    local_pts, shot_count, samples = traces.shape
    freq_count = freq_bins.shape[0]
    band_count = lax.axis_size("band")
    slab_count = lax.axis_size("slab")
    first_point = (lax.axis_index("slab") * band_count + lax.axis_index("band")) * local_pts
    in_kernel = (
        slab_count == 8
        and band_count == 4
        and freq_count == band_count
        and local_pts == 2 * LANES
        and shot_count == LANES
        and samples == 2 * LANES
        and data_matrix.shape[-1] == band_count * local_pts
    )
    if in_kernel:
        combined = predict(traces, data_matrix, shot_points, freq_bins, slab_count)
        return inverse(combined, freq_bins, samples)
    cosines, sines = tables(freq_bins, samples, 1.0 / math.sqrt(samples))
    forward_table = (
        jnp.transpose(jnp.stack([cosines, sines], -1), (1, 0, 2))
        .reshape(samples, 2 * freq_count)
        .astype(jnp.bfloat16)
    )
    points = first_point + jnp.arange(local_pts, dtype=jnp.int32)
    distance = (points[:, None] - shot_points[None, :]).astype(jnp.float32) / (NK / 8.0)
    aperture = 1.0 / (1.0 + distance * distance)
    transformed = jnp.dot(
        traces.reshape(local_pts * shot_count, samples), forward_table, preferred_element_type=jnp.float32
    )
    transformed = (
        transformed.reshape(local_pts, shot_count, freq_count, 2) * aperture[:, :, None, None]
    )
    cosines, sines = tables(freq_bins, samples, 1.0 / math.sqrt(2.0 * freq_count))
    inverse_table = jnp.stack([cosines, sines], 1).reshape(2 * freq_count, samples).astype(jnp.bfloat16)
    spectra = (
        jnp.transpose(transformed, (0, 2, 3, 1))
        .reshape(local_pts, freq_count, 2 * shot_count)
        .astype(jnp.bfloat16)
    )
    banded = lax.all_to_all(spectra, "band", split_axis=1, concat_axis=0, tiled=True)
    first_order = contract(banded, data_matrix).astype(jnp.bfloat16)
    second_order = contract(first_order, data_matrix)
    combined = (second_order - first_order.astype(jnp.float32)).astype(jnp.bfloat16)
    regrouped = lax.all_to_all(combined, "band", split_axis=0, concat_axis=1, tiled=True)
    regrouped = jnp.transpose(
        regrouped.reshape(local_pts, freq_count, 2, shot_count), (0, 3, 1, 2)
    ).reshape(local_pts * shot_count, 2 * freq_count)
    multiples = jnp.dot(regrouped, inverse_table, preferred_element_type=jnp.float32)
    return multiples.reshape(local_pts, shot_count, samples).astype(jnp.bfloat16)


def solution(mesh):
    placed = (P(("slab", "band"), None, None), P("band", None, None, "slab"), P(), P())
    return jax.shard_map(
        local,
        mesh=mesh,
        in_specs=placed,
        out_specs=P(("slab", "band"), None, None),
        check_vma=False,
    )
```
